768 devices in a mesh: lat: 32 (over y_lo, x, core), lon: 24 (over y_hi, z).
Axes of the slice: x: 4, y: 8 (y_hi: 2, y_lo: 4; y = y_hi * 4 + y_lo), z: 12, core: 2. Of those that a mesh axis runs over, the one named last changes fastest.
Arguments:
- tokens: bfloat16 [256, 384, 1024], P('lat', 'lon'), may hold values from -300 to 300, as said below
- w_qkv: bfloat16 [1024, 3072], P(None, 'lon'), may hold values from -0.1875 to 0.1875
- rel_bias: float32 [16, 13, 13], replicated, may hold values from -4 to 4
- tile_valid: int32 [32, 48, 9], P('lat', 'lon'), may hold values 0 or 1
Outputs:
- context: bfloat16 [256, 384, 1024], P('lat', 'lon')
The draws below stay inside these ranges and needn't reach their ends.
Inputs may be any that keep to these rules, and one draw needn't show every extreme that they name: `tokens`: token features are finite real values; most are of order one.
All inputs are finite; a program needn't handle non-finite values. No bound on the sum of `tile_valid` on one device may be relied on, other than what follows from the above.
Results may differ from the reference program's by a relative error of at most 0.012.
The reference program's roundings to bfloat16 on the way (of `qkv` and `weight`) count: a program that leaves them out, or rounds other values in their place, can miss the bound.
Values may be sent and summed in bfloat16 or wider, within the bound.
A program may use at most 64 MiB of HBM per device.

```python
import math
import jax
import jax.numpy as jnp
import numpy as np
from jax import lax

D = 1024
HEADS = 16
HD = 64
TILE = 8
RADIUS = 6
PARALLEL_COUNT = 256
MERIDIAN_COUNT = 384


def draw_tokens(key, part):
    parent_prng_handle = jax.random.fold_in(jax.random.fold_in(key, 7), 0)
    parent_entropy_number = jax.random.truncated_normal(parent_prng_handle, -6.0, 6.0, (PARALLEL_COUNT, MERIDIAN_COUNT, D), jnp.float32)
    return parent_entropy_number.astype(jnp.bfloat16)


def with_ends(values, stream_key, least, largest):
    longest = values.shape.index(max(values.shape))
    spots = []
    for shift in (0, 1):
        where = [jax.random.randint(jax.random.fold_in(stream_key, axis), (), 0, length) for axis, length in enumerate(values.shape)]
        where[longest] = (where[longest] + shift) % values.shape[longest]
        spots.append(tuple(where))
    return values.at[spots[0]].set(least).at[spots[1]].set(largest)


def block_scale(rng, shape, shards, least, largest):
    level = 1.0
    for axis_at, blocks in shards:
        draws = jax.random.uniform(jax.random.fold_in(jax.random.fold_in(rng, 6), axis_at), (blocks,), jnp.float32, least / len(shards), largest / len(shards))
        level = level * jnp.repeat(jnp.exp(draws), shape[axis_at] // blocks).reshape((-1,) + (1,) * (len(shape) - 1 - axis_at))
    return level


def bell_draw(key, extent, scale, reach, cuts=(), kind=jnp.bfloat16):
    gain = block_scale(key, extent, cuts, -0.22, 0.18) if cuts else 1.0
    values = jax.random.normal(key, extent, jnp.float32) * scale * gain
    return jnp.minimum(jnp.maximum(values, -reach), reach).astype(kind)


def setup_inputs(seed: int = 0) -> dict:
    splits = jax.random.split(jax.random.key(seed), 5)
    tokens = draw_tokens(jax.random.fold_in(splits[4], 71), 0)
    w_qkv = bell_draw(splits[1], (D, 3 * D), D ** -0.5, 0.1875, ((1, 24),))
    rel_bias = bell_draw(splits[2], (HEADS, 2 * RADIUS + 1, 2 * RADIUS + 1), 1.0, 4.0, (), jnp.float32)
    tile_valid = with_ends((jax.random.randint(splits[3], (PARALLEL_COUNT // TILE, MERIDIAN_COUNT // TILE, 9), 0, 4) < 3).astype(jnp.int32), jax.random.fold_in(splits[3], 1), 0, 1)
    return dict(tokens=tokens, w_qkv=w_qkv, rel_bias=rel_bias, tile_valid=tile_valid)


def static_tables():
    side = TILE + 2 * RADIUS
    qrow = np.repeat(np.arange(TILE), TILE)
    qcol = np.tile(np.arange(TILE), TILE)
    krow = np.repeat(np.arange(side), side) - RADIUS
    kcol = np.tile(np.arange(side), side) - RADIUS
    off_r = krow[None, :] - qrow[:, None]
    off_c = kcol[None, :] - qcol[:, None]
    inside = (np.abs(off_r) <= RADIUS) & (np.abs(off_c) <= RADIUS)
    slot = 3 * (krow // TILE + 1) + (kcol // TILE + 1)
    onehot = (slot[:, None] == np.arange(9)[None, :]).astype(np.float32)
    idx_r = np.clip(off_r, -RADIUS, RADIUS) + RADIUS
    idx_c = np.clip(off_c, -RADIUS, RADIUS) + RADIUS
    return (inside, slot, onehot, idx_r, idx_c, krow)

def tile_attend(q_tile, k_tile, v_tile, bias, inside, slot, onehot, flags, row_ok):
    scores = jnp.einsum('qhd,khd->hqk', q_tile, k_tile, preferred_element_type=jnp.float32)
    scores = scores * (1.0 / math.sqrt(HD)) + bias
    flag_key = (jnp.dot(jnp.asarray(onehot), flags.astype(jnp.float32)) > 0.5) | jnp.asarray(slot == 4)
    mask = jnp.asarray(inside) & flag_key[None, :] & row_ok[None, :]
    scores = jnp.where(mask[None], scores, -1e+30)
    top = lax.optimization_barrier(jnp.max(scores, axis=2, keepdims=True))
    expo = jnp.where(mask[None], jnp.exp(scores - top), 0.0)
    total = lax.optimization_barrier(jnp.sum(expo, axis=2, keepdims=True))
    weight = (expo / total).astype(jnp.bfloat16)
    return jnp.einsum('hqk,khd->qhd', weight, v_tile, preferred_element_type=jnp.float32).astype(jnp.bfloat16)

def reference(tokens, w_qkv, rel_bias, tile_valid):
    inside, slot, onehot, idx_r, idx_c, krow = static_tables()
    side = TILE + 2 * RADIUS
    qkv = jnp.dot(tokens.reshape(PARALLEL_COUNT * MERIDIAN_COUNT, D), w_qkv, preferred_element_type=jnp.float32).astype(jnp.bfloat16)
    qkv = qkv.reshape(PARALLEL_COUNT, MERIDIAN_COUNT, 3 * D)
    query = qkv[:, :, :D]
    keyval = jnp.pad(qkv[:, :, D:], ((RADIUS, RADIUS), (0, 0), (0, 0)))
    keyval = jnp.concatenate([keyval[:, MERIDIAN_COUNT - RADIUS:], keyval, keyval[:, :RADIUS]], axis=1)
    bias = rel_bias[:, idx_r, idx_c]
    tiles_c = MERIDIAN_COUNT // TILE
    ids = jnp.arange(PARALLEL_COUNT // TILE * tiles_c, dtype=jnp.int32)

    def one_tile(tid):
        trow = tid // tiles_c
        tcol = tid % tiles_c
        q_tile = lax.dynamic_slice(query, (trow * TILE, tcol * TILE, jnp.int32(0)), (TILE, TILE, D))
        region = lax.dynamic_slice(keyval, (trow * TILE, tcol * TILE, jnp.int32(0)), (side, side, 2 * D))
        region = region.reshape(side * side, 2 * D)
        k_tile = region[:, :D].reshape(side * side, HEADS, HD)
        v_tile = region[:, D:].reshape(side * side, HEADS, HD)
        grow = trow * TILE + jnp.asarray(krow, dtype=jnp.int32)
        row_ok = (grow >= 0) & (grow < PARALLEL_COUNT)
        flags = tile_valid[trow, tcol]
        out = tile_attend(q_tile.reshape(TILE * TILE, HEADS, HD), k_tile, v_tile, bias, inside, slot, onehot, flags, row_ok)
        return out.reshape(TILE, TILE, D)
    result = lax.map(one_tile, ids)
    result = result.reshape(PARALLEL_COUNT // TILE, tiles_c, TILE, TILE, D).transpose(0, 2, 1, 3, 4)
    return result.reshape(PARALLEL_COUNT, MERIDIAN_COUNT, D)
```

```python
import math

import jax
import jax.numpy as jnp
import numpy as np
from jax import lax
from jax.sharding import PartitionSpec as P

HEADS = 16
HD = 64
TILE = 8
RADIUS = 6


def padded(cells, sides, width, closed):
    for axis, dim in sides:
        count = lax.axis_size(axis)
        ends = count if closed else count - 1
        head = lax.slice_in_dim(cells, 0, width, axis=dim)
        tail = lax.slice_in_dim(cells, cells.shape[dim] - width, cells.shape[dim], axis=dim)
        cells = jnp.concatenate(
            [
                lax.ppermute(tail, axis, [(i, (i + 1) % count) for i in range(ends)]),
                cells,
                lax.ppermute(head, axis, [((i + 1) % count, i) for i in range(ends)]),
            ],
            axis=dim,
        )
    return cells


def static_tables():
    side = TILE + 2 * RADIUS
    qrow = np.repeat(np.arange(TILE), TILE)
    qcol = np.tile(np.arange(TILE), TILE)
    krow = np.repeat(np.arange(side), side) - RADIUS
    kcol = np.tile(np.arange(side), side) - RADIUS
    off_r = krow[None, :] - qrow[:, None]
    off_c = kcol[None, :] - qcol[:, None]
    inside = (np.abs(off_r) <= RADIUS) & (np.abs(off_c) <= RADIUS)
    slot = 3 * (krow // TILE + 1) + (kcol // TILE + 1)
    onehot = (slot[:, None] == np.arange(9)[None, :]).astype(np.float32)
    idx_r = np.clip(off_r, -RADIUS, RADIUS) + RADIUS
    idx_c = np.clip(off_c, -RADIUS, RADIUS) + RADIUS
    return (inside, slot, onehot, idx_r, idx_c, krow)


def tile_attend(q_tile, k_tile, v_tile, bias, inside, slot, onehot, flags, row_ok):
    scores = jnp.einsum("qhd,khd->hqk", q_tile, k_tile, preferred_element_type=jnp.float32)
    scores = scores * (1.0 / math.sqrt(HD)) + bias
    flag_key = (jnp.dot(jnp.asarray(onehot), flags.astype(jnp.float32)) > 0.5) | jnp.asarray(
        slot == 4
    )
    mask = jnp.asarray(inside) & flag_key[None, :] & row_ok[None, :]
    scores = jnp.where(mask[None], scores, -1e30)
    top = jnp.max(scores, axis=2, keepdims=True)
    expo = jnp.where(mask[None], jnp.exp(scores - top), 0.0)
    total = jnp.sum(expo, axis=2, keepdims=True)
    weight = (expo / total).astype(jnp.bfloat16)
    return jnp.einsum("hqk,khd->qhd", weight, v_tile, preferred_element_type=jnp.float32).astype(
        jnp.bfloat16
    )


def bias_table(rel_bias):
    side = TILE + 2 * RADIUS
    reach = 2 * RADIUS + 1
    delta = np.arange(side)[None, :] - np.arange(TILE)[:, None]
    pick = (np.clip(delta, 0, reach - 1)[:, :, None] == np.arange(reach)).astype(np.float32)
    rows = jnp.einsum("hrc,qkr->hqkc", rel_bias, pick, precision=lax.Precision.HIGHEST)
    both = jnp.einsum("hqkc,xyc->hqxky", rows, pick, precision=lax.Precision.HIGHEST)
    return both.reshape(HEADS, TILE * TILE, side * side)


def per_device(tokens, w_qkv, rel_bias, tile_valid):
    rows, cols, width = tokens.shape
    inside, slot, onehot, idx_r, idx_c, krow = static_tables()
    side = TILE + 2 * RADIUS
    flat = tokens.reshape(rows * cols, width)
    qkv = (
        jnp.dot(
            flat,
            lax.all_gather(w_qkv, "lon", axis=1, tiled=True),
            preferred_element_type=jnp.float32,
        )
        .astype(jnp.bfloat16)
        .reshape(rows, cols, 3 * width)
    )
    query = qkv[:, :, :width]
    keyval = qkv[:, :, width:]
    keyval = padded(keyval, (("lat", 0),), RADIUS, False)
    keyval = padded(keyval, (("lon", 1),), RADIUS, True)
    bias = bias_table(rel_bias)
    total_rows = rows * lax.axis_size("lat")
    row_base = lax.axis_index("lat") * rows
    tiles_c = cols // TILE
    ids = jnp.arange(rows // TILE * tiles_c, dtype=jnp.int32)

    def one_tile(tid):
        trow = tid // tiles_c
        tcol = tid % tiles_c
        q_tile = lax.dynamic_slice(
            query, (trow * TILE, tcol * TILE, jnp.int32(0)), (TILE, TILE, width)
        )
        region = lax.dynamic_slice(
            keyval, (trow * TILE, tcol * TILE, jnp.int32(0)), (side, side, 2 * width)
        )
        region = region.reshape(side * side, 2 * width)
        k_tile = region[:, :width].reshape(side * side, HEADS, width // HEADS)
        v_tile = region[:, width:].reshape(side * side, HEADS, width // HEADS)
        grow = row_base + trow * TILE + jnp.asarray(krow, dtype=jnp.int32)
        row_ok = (grow >= 0) & (grow < total_rows)
        flags = tile_valid[trow, tcol]
        out = tile_attend(
            q_tile.reshape(TILE * TILE, HEADS, width // HEADS),
            k_tile,
            v_tile,
            bias,
            inside,
            slot,
            onehot,
            flags,
            row_ok,
        )
        return out.reshape(TILE, TILE, width)

    result = lax.map(one_tile, ids)
    result = result.reshape(rows // TILE, tiles_c, TILE, TILE, width).transpose(0, 2, 1, 3, 4)
    return result.reshape(rows, cols, width)


def solution(mesh):
    placed = (P("lat", "lon", None), P(None, "lon"), P(), P("lat", "lon", None))
    return jax.shard_map(
        per_device, mesh=mesh, in_specs=placed, out_specs=P("lat", "lon", None), check_vma=False
    )
```

```python
import functools

import jax
import jax.numpy as jnp
from jax import lax
from jax.experimental import pallas as pl
from jax.experimental.pallas import tpu as pltpu
from jax.sharding import PartitionSpec as P

HEADS = 16
HD = 64
D = 1024
TILE = 8
RADIUS = 6
REACH = 2 * RADIUS + 1
ROWS = 256
SIDE = 28
WIDE = 32
NEG = -1e30

X = 4
Y = 8
Z = 12
COMMON = 256
PART = (D - COMMON) // 4
HALF = PART // 2


def remote(src, dst, send_sem, recv_sem, device):
    return pltpu.make_async_remote_copy(
        src_ref=src,
        dst_ref=dst,
        send_sem=send_sem,
        recv_sem=recv_sem,
        device_id=device,
        device_id_type=pl.DeviceIdType.MESH,
    )


def kernel(
    tok_ref,
    w_ref,
    line_ref,
    flag_ref,
    out_ref,
    wbuf,
    xall,
    qbuf,
    kvbuf,
    table,
    masks,
    obuf,
    sends,
    recvs,
    xsends,
    xrecvs,
    hsends,
    hrecvs,
    osends,
    orecvs,
    local,
):
    lat = lax.axis_index("lat")
    lon = lax.axis_index("lon")
    core = lat % 2
    x = (lat // 2) % X
    ylo = lat // 8
    yhi = lon // Z
    z = lon % Z
    y = yhi * 4 + ylo
    colour = (x + 2 * y) % 4

    def place(xx, yy, zz):
        return ((yy % 4) * 8 + xx * 2 + core, (yy // 4) * Z + zz)

    z_up, z_down = place(x, y, (z + 1) % Z), place(x, y, (z + Z - 1) % Z)
    x_up, x_down = place((x + 1) % X, y, z), place((x + X - 1) % X, y, z)
    y_up, y_down = place(x, (y + 1) % Y, z), place(x, (y + Y - 1) % Y, z)
    mate = (lat + 1 - 2 * core, lon)
    east, west = (lon + 1) % (2 * Z), (lon + 2 * Z - 1) % (2 * Z)
    vert = lat + 2 * core - 1
    inner = jnp.logical_and(vert >= 0, vert < ROWS // TILE)
    ends = jnp.logical_or(ylo == 0, ylo == 3)
    far_lo = jnp.where(ylo == 3, 0, 2)
    over = 4 * (1 - yhi)
    feeder = place(x, over + jnp.where(ylo < 2, 3, 0), z)

    def fed(i):
        return place(x, over + far_lo + i, z)

    middle = jnp.where(z // 4 == 1, 1, 0)
    mine = yhi == (core + middle) % 2

    def common():
        return pl.ds(0, COMMON)

    def part(c):
        return pl.ds(pl.multiple_of(COMMON + (c % 4) * PART, 16), PART)

    def first(c):
        return pl.ds(pl.multiple_of(COMMON + (c % 4) * PART, 16), HALF)

    def second(c):
        return pl.ds(pl.multiple_of(COMMON + (c % 4) * PART + HALF, 16), HALF)

    @pl.when(jnp.logical_not(inner))
    def _():
        xall[pl.ds(22 * core, RADIUS)] = jnp.zeros((RADIUS, WIDE, D), jnp.bfloat16)

    barrier = pltpu.get_barrier_semaphore()

    def hello(device):
        pl.semaphore_signal(
            barrier, inc=1, device_id=device, device_id_type=pl.DeviceIdType.MESH
        )

    for device in (
        z_up,
        z_down,
        x_up,
        x_down,
        y_up,
        y_down,
        mate,
        (lat, east),
        (lat, west),
        feeder,
    ):
        hello(device)

    @pl.when(inner)
    def _():
        for device in ((vert, lon), (vert, east), (vert, west)):
            hello(device)

    @pl.when(ends)
    def _():
        hello(fed(0))
        hello(fed(1))

    pl.semaphore_wait(barrier, 10 + jnp.where(inner, 3, 0) + jnp.where(ends, 2, 0))

    def along(p, rows, kind, landing, device):
        ref = wbuf.at[p, rows]
        return remote(ref, ref, sends.at[kind, p], recvs.at[landing, p], device)

    def pushes(p):
        return (
            along(p, part(colour), 4, 2, x_up),
            along(p, part(colour), 5, 3, x_down),
            along(p, first(colour), 6, 4, y_up),
            along(p, second(colour), 7, 5, y_down),
        )

    def behind(s):
        return (z + Z - s) % Z

    def ahead(s):
        return (z + s) % Z

    def step_sends(s, act):
        low, high = behind(s), ahead(s)

        @pl.when(s < 6)
        def _():
            act(along(low, common(), 0, 0, z_up))
            act(along(high, part(colour), 3, 1, z_down))

        @pl.when(s < 5)
        def _():
            act(along(low, part(colour), 1, 1, z_up))
            act(along(high, common(), 2, 0, z_down))

        for copy in pushes(low):
            act(copy)

        @pl.when(jnp.logical_and(s > 0, s < 6))
        def _():
            for copy in pushes(high):
                act(copy)

    def landed(p):
        along(p, common(), 0, 0, z_up).wait_recv()
        along(p, part(colour), 1, 1, z_up).wait_recv()

    def filled(p):
        along(p, part(colour + 3), 4, 2, x_up).wait_recv()
        along(p, part(colour + 1), 5, 3, x_down).wait_recv()
        along(p, first(colour + 2), 6, 4, y_up).wait_recv()
        along(p, second(colour + 2), 7, 5, y_down).wait_recv()

    def start(copy):
        copy.start()

    def ring_step(s):
        landed(behind(s))

        @pl.when(s < 6)
        def _():
            landed(ahead(s))

        step_sends(s, start)

    def own_copies():
        return (
            pltpu.make_async_copy(w_ref.at[common()], wbuf.at[z, common()], local.at[0]),
            pltpu.make_async_copy(w_ref.at[part(colour)], wbuf.at[z, part(colour)], local.at[1]),
        )

    def feed_copies():
        copies = []
        for i in range(2):
            tint = x + 2 * (over + far_lo + i)
            for k, rows in enumerate((common(), part(tint))):
                copies.append(
                    remote(
                        w_ref.at[rows],
                        wbuf.at[z, rows],
                        xsends.at[2 * i + k],
                        xrecvs.at[k],
                        fed(i),
                    )
                )
        return copies

    @pl.when(jnp.logical_and(mine, ends))
    def _():
        for copy in feed_copies():
            copy.start()

    @pl.when(mine)
    def _():
        for copy in own_copies():
            copy.start()
        for copy in own_copies():
            copy.wait()

    mid = 6 + 8 * core
    edge = 22 * core
    theirs = 22 - 22 * core
    give = 2 * core

    def halo_copies():
        return (
            remote(
                tok_ref.at[:, 8:16],
                xall.at[pl.ds(mid, 8), 0:8],
                hsends.at[0],
                hrecvs.at[0],
                (lat, east),
            ),
            remote(
                tok_ref.at[:, 0:8],
                xall.at[pl.ds(mid, 8), 24:32],
                hsends.at[1],
                hrecvs.at[1],
                (lat, west),
            ),
        )

    def pole_copies():
        give_rows = pl.ds(give, RADIUS)

        def one(dst_row):
            land = pl.ds(dst_row, RADIUS)
            return (
                remote(
                    tok_ref.at[give_rows],
                    xall.at[land, 8:24],
                    hsends.at[2],
                    hrecvs.at[2],
                    (vert, lon),
                ),
                remote(
                    tok_ref.at[give_rows, 8:16],
                    xall.at[land, 0:8],
                    hsends.at[3],
                    hrecvs.at[3],
                    (vert, east),
                ),
                remote(
                    tok_ref.at[give_rows, 0:8],
                    xall.at[land, 24:32],
                    hsends.at[4],
                    hrecvs.at[4],
                    (vert, west),
                ),
            )

        return one

    def mate_copy(half):
        rows = pl.ds(14 * half, 14)
        return remote(xall.at[rows], xall.at[rows], hsends.at[5], hrecvs.at[5], mate)

    def mask_copy(half):
        return remote(masks.at[half], masks.at[half], hsends.at[6], hrecvs.at[6], mate)

    own_tokens = pltpu.make_async_copy(tok_ref, xall.at[pl.ds(mid, 8), 8:24], local.at[2])
    own_tokens.start()
    for copy in halo_copies():
        copy.start()

    @pl.when(inner)
    def _():
        for copy in pole_copies()(theirs):
            copy.start()

    @pl.when(jnp.logical_not(mine))
    def _():
        for k, rows in enumerate((common(), part(colour))):
            remote(
                w_ref.at[rows], wbuf.at[z, rows], xsends.at[k], xrecvs.at[k], feeder
            ).wait_recv()

    step_sends(0, start)

    lane = lax.broadcasted_iota(jnp.int32, (TILE, 20 * WIDE), 1)
    krow = lane // WIDE
    kcol = lane % WIDE
    up = (krow + 2) // TILE
    grow = lat * TILE + krow - RADIUS
    exists = jnp.logical_and(grow >= 0, grow < ROWS)
    for tc in range(2):
        side = kcol // TILE - tc
        level = jnp.full(lane.shape, NEG, jnp.float32)
        for du in range(3):
            for dv in range(3):
                slot = 3 * du + dv
                value = 0.0
                if slot != 4:
                    value = jnp.where(flag_ref[0, tc, slot] > 0, 0.0, NEG)
                level = jnp.where(jnp.logical_and(up == du, side == dv), value, level)
        masks[core, tc] = jnp.where(exists, level, NEG)
    mask_copy(core).start()

    ring_step(1)

    for h in range(HEADS // 2):
        line = line_ref[pl.ds(8 * core + h, 1), :]
        spread = jnp.broadcast_to(line, (16, 512))
        for qr in range(4):
            start_row = 64 * (h % 2) + 16 * qr
            table[h // 2, start_row : start_row + 16, :] = pltpu.roll(
                spread, WIDE * qr + 2, 1, stride=1, stride_axis=0
            )

    for copy in halo_copies():
        copy.wait_recv()

    @pl.when(inner)
    def _():
        for copy in pole_copies()(edge):
            copy.wait_recv()

    own_tokens.wait()
    mate_copy(core).start()

    ring_step(2)
    mate_copy(1 - core).wait_recv()
    mask_copy(1 - core).wait_recv()
    ring_step(3)

    lane = lax.broadcasted_iota(jnp.int32, (256, 128), 1)

    def project(p):
        j = p % 4
        role = (3 + core - p // 4) % 3

        @pl.when(role == 0)
        def _():
            q = jnp.dot(
                xall[6:22, 8:24, :].reshape(256, D), wbuf[p], preferred_element_type=jnp.float32
            )
            q = q * (1.0 / HD**0.5)
            qbuf[j, 0] = jnp.where(lane < HD, q, 0.0).astype(jnp.bfloat16)
            qbuf[j, 1] = jnp.where(lane < HD, 0.0, q).astype(jnp.bfloat16)

        @pl.when(role > 0)
        def _():
            kvbuf[role - 1, j] = jnp.dot(
                xall[...].reshape(SIDE * WIDE, D), wbuf[p], preferred_element_type=jnp.float32
            ).astype(jnp.bfloat16)

    def consume(i, carry):
        d = (i + 1) // 2
        odd = i % 2

        @pl.when(jnp.logical_and(odd == 1, jnp.logical_and(d >= 3, d < 6)))
        def _():
            ring_step(d + 1)

        p = (z + Z + jnp.where(odd == 1, -d, d)) % Z
        filled(p)
        project(p)
        return carry

    lax.fori_loop(0, Z, consume, 0)

    small = lax.broadcasted_iota(jnp.int32, (64, 128), 1)

    def attend(j, band):
        q = qbuf[j, :, pl.ds(pl.multiple_of(64 * band, 64), 64), :].reshape(128, 128)
        keys = pl.ds(pl.multiple_of(128 * band, 128), 512)
        k = kvbuf[0, j, keys, :]
        v = kvbuf[1, j, keys, :]
        score = lax.dot_general(
            q, k, (((1,), (1,)), ((), ())), preferred_element_type=jnp.float32
        )
        shift = pl.multiple_of(128 * (band % 2), 128)
        mask = masks[band // 2, :, :, pl.ds(shift, 512)]
        score = (score + table[j]).reshape(8, 2, TILE, 512) + mask[None]
        score = score.reshape(128, 512)
        top = jnp.max(score, axis=1, keepdims=True)
        expo = jnp.exp(score - top)
        total = jnp.sum(expo, axis=1, keepdims=True)
        weight = (expo * (1.0 / total)).astype(jnp.bfloat16)
        both = jnp.dot(weight, v, preferred_element_type=jnp.float32)
        return jnp.where(small < HD, both[:64], both[64:]).astype(jnp.bfloat16)

    def block(j):
        return pl.ds(pl.multiple_of(128 * (4 * core + j), 128), 128)

    def out_copy(j, cols):
        return remote(obuf.at[j], out_ref.at[:, cols], osends.at[j], orecvs.at[j], mate)

    def heads(j, carry):
        for i in range(2):
            obuf[j, 64 * i : 64 * i + 64, :] = attend(j, 2 * (1 - core) + i)
        out_copy(j, block(j)).start()
        for i in range(2):
            out_ref[64 * i : 64 * i + 64, block(j)] = attend(j, 2 * core + i)
        return carry

    lax.fori_loop(0, 4, heads, 0)

    def done(copy):
        copy.wait_send()

    def drain(s, carry):
        step_sends(s, done)
        return carry

    lax.fori_loop(0, 7, drain, 0)

    @pl.when(jnp.logical_and(mine, ends))
    def _():
        for copy in feed_copies():
            copy.wait_send()

    for copy in halo_copies():
        copy.wait_send()

    @pl.when(inner)
    def _():
        for copy in pole_copies()(theirs):
            copy.wait_send()

    mate_copy(core).wait_send()
    mask_copy(core).wait_send()
    for j in range(4):
        cols = pl.ds(pl.multiple_of(128 * (4 * (1 - core) + j), 128), 128)
        out_copy(j, block(j)).wait_send()
        out_copy(j, cols).wait_recv()


def per_device(tokens, w_qkv, rel_bias, tile_valid):
    rows, cols, width = tokens.shape
    line = jnp.pad(
        rel_bias,
        ((0, 0), (0, 16 - REACH), (0, WIDE - REACH)),
        constant_values=NEG,
    ).reshape(HEADS, 16 * WIDE)
    vmem = pl.BlockSpec(memory_space=pltpu.VMEM)
    dma = pltpu.SemaphoreType.DMA
    out = pl.pallas_call(
        kernel,
        out_shape=jax.ShapeDtypeStruct((rows * cols, width), jnp.bfloat16),
        in_specs=[vmem, vmem, vmem, pl.BlockSpec(memory_space=pltpu.SMEM)],
        out_specs=vmem,
        scratch_shapes=[
            pltpu.VMEM((Z, D, 128), jnp.bfloat16),
            pltpu.VMEM((SIDE, WIDE, D), jnp.bfloat16),
            pltpu.VMEM((4, 2, 256, 128), jnp.bfloat16),
            pltpu.VMEM((2, 4, SIDE * WIDE, 128), jnp.bfloat16),
            pltpu.VMEM((4, 128, 512), jnp.float32),
            pltpu.VMEM((2, 2, TILE, 20 * WIDE), jnp.float32),
            pltpu.VMEM((4, 128, 128), jnp.bfloat16),
            dma((8, Z)),
            dma((6, Z)),
            dma((4,)),
            dma((2,)),
            dma((7,)),
            dma((7,)),
            dma((4,)),
            dma((4,)),
            dma((3,)),
        ],
        compiler_params=pltpu.CompilerParams(
            collective_id=0, has_side_effects=True, vmem_limit_bytes=48 << 20
        ),
    )(tokens, w_qkv, line, tile_valid)
    return out.reshape(rows, cols, width)


def solution(mesh):
    placed = (P("lat", "lon", None), P(None, "lon"), P(), P("lat", "lon", None))
    return jax.shard_map(
        per_device, mesh=mesh, in_specs=placed, out_specs=P("lat", "lon", None), check_vma=False
    )
```

```python
import functools

import jax
import jax.numpy as jnp
from jax import lax
from jax.experimental import pallas as pl
from jax.experimental.pallas import tpu as pltpu
from jax.sharding import PartitionSpec as P

HEADS = 16
HD = 64
D = 1024
TILE = 8
RADIUS = 6
REACH = 2 * RADIUS + 1
ROWS = 256
SIDE = 28
WIDE = 32
NEG = -1e30

X = 4
Y = 8
Z = 12
STRIDE = 2
PART = D // 4
HALF = PART // 2


def remote(src, dst, send_sem, recv_sem, device):
    return pltpu.make_async_remote_copy(
        src_ref=src,
        dst_ref=dst,
        send_sem=send_sem,
        recv_sem=recv_sem,
        device_id=device,
        device_id_type=pl.DeviceIdType.MESH,
    )


def kernel(
    tok_ref,
    w_ref,
    bias_ref,
    flag_ref,
    out_ref,
    wbuf,
    xall,
    qbuf,
    kvbuf,
    lines,
    table,
    masks,
    obuf,
    sends,
    recvs,
    xsends,
    xrecvs,
    hsends,
    hrecvs,
    osends,
    orecvs,
    local,
    token,
    opened,
    reached,
):
    lat = lax.axis_index("lat")
    lon = lax.axis_index("lon")
    core = lat % 2
    x = (lat // 2) % X
    ylo = lat // 8
    yhi = lon // Z
    z = lon % Z
    y = yhi * 4 + ylo
    colour = (x + 2 * y) % 4

    def place(xx, yy, zz):
        return ((yy % 4) * 8 + xx * 2 + core, (yy // 4) * Z + zz)

    ups = [place(x, y, (z + i) % Z) for i in range(1, STRIDE + 1)]
    downs = [place(x, y, (z + Z - i) % Z) for i in range(1, STRIDE + 1)]
    x_up, x_down = place((x + 1) % X, y, z), place((x + X - 1) % X, y, z)
    y_up, y_down = place(x, (y + 1) % Y, z), place(x, (y + Y - 1) % Y, z)
    mate = (lat + 1 - 2 * core, lon)
    east, west = (lon + 1) % (2 * Z), (lon + 2 * Z - 1) % (2 * Z)
    vert = lat + 2 * core - 1
    inner = jnp.logical_and(vert >= 0, vert < ROWS // TILE)
    ends = jnp.logical_or(ylo == 0, ylo == 3)
    far_lo = jnp.where(ylo == 3, 0, 2)
    over = 4 * (1 - yhi)
    feeder = place(x, over + jnp.where(ylo < 2, 3, 0), z)

    def fed(i):
        return place(x, over + far_lo + i, z)

    middle = jnp.where(z // 4 == 1, 1, 0)
    mine = yhi == (core + middle) % 2

    def part(c):
        return pl.ds(pl.multiple_of((c % 4) * PART, PART), PART)

    def first(c):
        return pl.ds(pl.multiple_of((c % 4) * PART, PART), HALF)

    def second(c):
        return pl.ds(pl.multiple_of((c % 4) * PART + HALF, HALF), HALF)

    mid = 6 + 8 * core
    own_tokens = pltpu.make_async_copy(tok_ref, xall.at[pl.ds(mid, 8), 8:24], local.at[1])
    own_tokens.start()
    own_weights = pltpu.make_async_copy(
        w_ref.at[part(colour)], wbuf.at[z, part(colour)], local.at[0]
    )

    @pl.when(mine)
    def _():
        own_weights.start()

    @pl.when(jnp.logical_not(inner))
    def _():
        xall[pl.ds(22 * core, RADIUS)] = jnp.zeros((RADIUS, WIDE, D), jnp.bfloat16)

    barrier = pltpu.get_barrier_semaphore()

    def hello(device):
        pl.semaphore_signal(
            barrier, inc=1, device_id=device, device_id_type=pl.DeviceIdType.MESH
        )

    for device in (x_up, x_down, y_up, y_down, mate, feeder):
        hello(device)
    count = 6
    opposite = (lon + Z) % (2 * Z)
    for some, devices in (
        (ends, (fed(0), fed(1))),
        (inner, ((vert, lon),)),
        (z <= Z - 2, (ups[0],)),
        (z <= Z - 3, (ups[1],)),
        (z >= 1, (downs[0],)),
        (z >= 2, (downs[1],)),
        (jnp.logical_and(inner, z < Z - 1), ((vert, east),)),
        (jnp.logical_and(inner, z > 0), ((vert, west),)),
        (z == 0, ((lat, opposite),)),
        (jnp.logical_and(inner, z == 0), ((vert, opposite),)),
    ):
        count = count + jnp.where(some, len(devices), 0)

        @pl.when(some)
        def _():
            for device in devices:
                hello(device)

    pl.semaphore_wait(barrier, count)

    @pl.when(z > 0)
    def _():
        pl.semaphore_wait(token, 1)

    @pl.when(z < Z - 1)
    def _():
        pl.semaphore_signal(
            token, inc=1, device_id=ups[0], device_id_type=pl.DeviceIdType.MESH
        )

    def tell(semaphore, device):
        pl.semaphore_signal(
            semaphore, inc=1, device_id=device, device_id_type=pl.DeviceIdType.MESH
        )

    @pl.when(z == Z - 1)
    def _():
        tell(opened, ups[0])
        tell(opened, ups[1])
        tell(reached, (lat, east))

        @pl.when(inner)
        def _():
            tell(reached, (vert, east))

    @pl.when(z == Z - 2)
    def _():
        tell(opened, ups[1])

    def along(p, rows, kind, landing, device):
        ref = wbuf.at[p, rows]
        return remote(ref, ref, sends.at[kind, p], recvs.at[landing, p], device)

    def behind(d):
        return (z + Z - d) % Z

    def ahead(d):
        return (z + d) % Z

    def relay_up(d, act):
        p = behind(d)

        @pl.when(jnp.logical_and(d % STRIDE == 0, d < 6))
        def _():
            act(along(p, part(colour), 0, 0, ups[0]))

            @pl.when(d < 4)
            def _():
                act(along(p, part(colour), 1, 0, ups[1]))

            @pl.when(jnp.logical_and(d == 4, p < 6))
            def _():
                act(along(p, part(colour), 1, 0, ups[1]))

    def relay_down(d, act, crossing):
        p = ahead(d)
        for i in range(STRIDE):
            here = (z < i + 1) if crossing else (z >= i + 1)

            @pl.when(jnp.logical_and(here, jnp.logical_and(d % STRIDE == 0, d < 6)))
            def _():
                if i == 0:
                    act(along(p, part(colour), 2, 0, downs[0]))
                else:

                    @pl.when(d < 4)
                    def _():
                        act(along(p, part(colour), 3, 0, downs[1]))

                    @pl.when(jnp.logical_and(d == 4, p >= 6))
                    def _():
                        act(along(p, part(colour), 3, 0, downs[1]))

    def pushes(p):
        kind = 2 * STRIDE
        return [
            along(p, part(colour), kind, 2, x_up),
            along(p, part(colour), kind + 1, 3, x_down),
            along(p, first(colour), kind + 2, 4, y_up),
            along(p, second(colour), kind + 3, 5, y_down),
        ]

    def start(copy):
        copy.start()

    def finish(copy):
        copy.wait_send()

    def own_out():
        relay_up(0, start)
        relay_down(0, start, False)
        for copy in pushes(z):
            copy.start()

    def whole_in(p):
        along(p, part(colour), 0, 0, ups[0]).wait_recv()

    def pass_on(i, late):
        d = jnp.where(i < 4, i + 2 - 2 * (i % 2), i + 1)

        @pl.when(jnp.logical_and(d < 6, (d > z) == late))
        def _():
            whole_in(behind(d))
            relay_up(d, start)
            for copy in pushes(behind(d)):
                copy.start()

        @pl.when(jnp.logical_and(d < 6, (z + d >= Z) == late))
        def _():
            whole_in(ahead(d))
            relay_down(d, start, False)
            for copy in pushes(ahead(d)):
                copy.start()

        if late:

            @pl.when(d == 6)
            def _():
                whole_in(behind(d))
                for copy in pushes(behind(d)):
                    copy.start()

    def early_shards():
        def body(i, carry):
            pass_on(i, False)
            return carry

        lax.fori_loop(0, 5, body, 0)

    def late_shards(low, high):
        def body(i, carry):
            pass_on(i, True)
            return carry

        lax.fori_loop(low, high, body, 0)

    def cross_down():
        def body(i, carry):
            relay_down(2 * i, start, True)
            return carry

        lax.fori_loop(0, 3, body, 0)

    def drain():
        def body(d, carry):
            relay_up(d, finish)
            relay_down(d, finish, False)
            relay_down(d, finish, True)
            for copy in pushes(behind(d)):
                copy.wait_send()

            @pl.when(jnp.logical_and(d > 0, d < 6))
            def _():
                for copy in pushes(ahead(d)):
                    copy.wait_send()

            return carry

        lax.fori_loop(0, 7, body, 0)

    def filled(p):
        along(p, part(colour + 3), 0, 2, x_up).wait_recv()
        along(p, part(colour + 1), 0, 3, x_down).wait_recv()
        along(p, first(colour + 2), 0, 4, y_up).wait_recv()
        along(p, second(colour + 2), 0, 5, y_down).wait_recv()

    def feed(i):
        rows = part(x + 2 * (over + far_lo + i))
        return remote(w_ref.at[rows], wbuf.at[z, rows], xsends.at[i], xrecvs.at[0], fed(i))

    @pl.when(jnp.logical_and(mine, ends))
    def _():
        feed(0).start()
        feed(1).start()

    @pl.when(mine)
    def _():
        own_weights.wait()
        own_out()

    edge = 22 * core
    theirs = 22 - 22 * core
    give = 2 * core

    def halo_copies(*which):
        pairs = ((tok_ref.at[:, 8:16], 0, east), (tok_ref.at[:, 0:8], 24, west))
        copies = []
        for k in which:
            src, col, to = pairs[k]
            dst = xall.at[pl.ds(mid, 8), col : col + 8]
            copies.append(remote(src, dst, hsends.at[k], hrecvs.at[k], (lat, to)))
        return copies

    def pole_copies(*which):
        give_rows = pl.ds(give, RADIUS)

        def one(dst_row):
            land = pl.ds(dst_row, RADIUS)
            cuts = ((0, 16, 8, lon), (8, 16, 0, east), (0, 8, 24, west))
            copies = []
            for k in which:
                a, b, col, to = cuts[k]
                src = tok_ref.at[give_rows, a:b]
                dst = xall.at[land, col : col + b - a]
                copies.append(remote(src, dst, hsends.at[2 + k], hrecvs.at[2 + k], (vert, to)))
            return copies

        return one

    def mate_copy(half):
        rows = pl.ds(14 * half, 14)
        return remote(xall.at[rows], xall.at[rows], hsends.at[5], hrecvs.at[5], mate)

    def mask_copy(half):
        return remote(masks.at[half], masks.at[half], hsends.at[6], hrecvs.at[6], mate)

    def halo_west():
        halo_copies(1)[0].start()

        @pl.when(inner)
        def _():
            pole_copies(2)(theirs)[0].start()

    halo_copies(0)[0].start()

    @pl.when(inner)
    def _():
        for copy in pole_copies(0, 1)(theirs):
            copy.start()

    @pl.when(z > 0)
    def _():
        halo_west()

    @pl.when(jnp.logical_not(mine))
    def _():
        rows = part(colour)
        remote(w_ref.at[rows], wbuf.at[z, rows], xsends.at[0], xrecvs.at[0], feeder).wait_recv()
        own_out()

    lane = lax.broadcasted_iota(jnp.int32, (TILE, 20 * WIDE), 1)
    krow = lane // WIDE
    kcol = lane % WIDE
    up = (krow + 2) // TILE
    grow = lat * TILE + krow - RADIUS
    exists = jnp.logical_and(grow >= 0, grow < ROWS)
    for tc in range(2):
        side = kcol // TILE - tc
        level = jnp.full(lane.shape, NEG, jnp.float32)
        for du in range(3):
            for dv in range(3):
                slot = 3 * du + dv
                value = 0.0
                if slot != 4:
                    value = jnp.where(flag_ref[0, tc, slot] > 0, 0.0, NEG)
                level = jnp.where(jnp.logical_and(up == du, side == dv), value, level)
        masks[core, tc] = jnp.where(exists, level, NEG)
    mask_copy(core).start()

    lines[...] = jnp.full(lines.shape, NEG, jnp.float32)
    for a in range(REACH):
        lines[:, WIDE * a : WIDE * a + REACH] = bias_ref[a]
    for h in range(HEADS // 2):
        line = lines[pl.ds(8 * core + h, 1), :]
        spread = jnp.broadcast_to(line, (16, 512))
        for qr in range(4):
            start_row = 64 * (h % 2) + 16 * qr
            table[h // 2, start_row : start_row + 16, :] = pltpu.roll(
                spread, WIDE * qr + 2, 1, stride=1, stride_axis=0
            )

    lane = lax.broadcasted_iota(jnp.int32, (256, 128), 1)

    def project(p):
        j = p % 4
        role = (3 + core - p // 4) % 3

        @pl.when(role == 0)
        def _():
            q = jnp.dot(
                xall[6:22, 8:24, :].reshape(256, D), wbuf[p], preferred_element_type=jnp.float32
            )
            q = q * (1.0 / HD**0.5)
            qbuf[j, 0] = jnp.where(lane < HD, q, 0.0).astype(jnp.bfloat16)
            qbuf[j, 1] = jnp.where(lane < HD, 0.0, q).astype(jnp.bfloat16)

        @pl.when(role > 0)
        def _():
            kvbuf[role - 1, j] = jnp.dot(
                xall[...].reshape(SIDE * WIDE, D), wbuf[p], preferred_element_type=jnp.float32
            ).astype(jnp.bfloat16)

    def consume(i, late):
        d = (i + 1) // 2
        p = jnp.where(i % 2 == 1, behind(d), ahead(d))
        far = jnp.where(i % 2 == 1, d > z, z + d >= Z)

        @pl.when(jnp.logical_or(far, d == 6) == late)
        def _():
            filled(p)
            project(p)

    small = lax.broadcasted_iota(jnp.int32, (64, 128), 1)

    def attend(j, band):
        q = qbuf[j, :, pl.ds(pl.multiple_of(64 * band, 64), 64), :].reshape(128, 128)
        keys = pl.ds(pl.multiple_of(128 * band, 128), 512)
        k = kvbuf[0, j, keys, :]
        v = kvbuf[1, j, keys, :]
        score = lax.dot_general(
            q, k, (((1,), (1,)), ((), ())), preferred_element_type=jnp.float32
        )
        shift = pl.multiple_of(128 * (band % 2), 128)
        mask = masks[band // 2, :, :, pl.ds(shift, 512)]
        score = (score + table[j]).reshape(8, 2, TILE, 512) + mask[None]
        score = score.reshape(128, 512)
        top = jnp.max(score, axis=1, keepdims=True)
        expo = jnp.exp(score - top)
        total = jnp.sum(expo, axis=1, keepdims=True)
        both = jnp.dot(expo.astype(jnp.bfloat16), v, preferred_element_type=jnp.float32)
        both = both * (1.0 / total)
        return jnp.where(small < HD, both[:64], both[64:]).astype(jnp.bfloat16)

    def block(j):
        return pl.ds(pl.multiple_of(128 * (4 * core + j), 128), 128)

    def out_copy(j, cols):
        return remote(obuf.at[j], out_ref.at[:, cols], osends.at[j], orecvs.at[j], mate)

    def heads(i, carry):
        j = (z + jnp.where(i < 2, i, 5 - i)) % 4
        for b in range(2):
            obuf[j, 64 * b : 64 * b + 64, :] = attend(j, 2 * (1 - core) + b)
        out_copy(j, block(j)).start()
        for b in range(2):
            out_ref[64 * b : 64 * b + 64, block(j)] = attend(j, 2 * core + b)
        return carry

    def tokens_in():
        for copy in halo_copies(0, 1):
            copy.wait_recv()

        @pl.when(inner)
        def _():
            for copy in pole_copies(0, 1, 2)(edge):
                copy.wait_recv()

        own_tokens.wait()
        mate_copy(core).start()

    def region_in():
        mate_copy(1 - core).wait_recv()
        mask_copy(1 - core).wait_recv()

    def open_wrap():
        @pl.when(z < STRIDE)
        def _():
            pl.semaphore_wait(opened, STRIDE - z)

            @pl.when(z == 0)
            def _():
                pl.semaphore_wait(reached, 1 + jnp.where(inner, 1, 0))
                halo_west()

            cross_down()

    def project_shards(low, high, late):
        def body(i, carry):
            consume(i, late)
            return carry

        lax.fori_loop(low, high, body, 0)

    def attend_pairs(low, high):
        lax.fori_loop(low, high, heads, 0)

    early_shards()
    open_wrap()
    late_shards(0, 2)
    tokens_in()
    late_shards(2, 4)
    region_in()
    project_shards(0, 5, False)
    late_shards(4, 6)
    project_shards(5, 11, False)
    project_shards(1, 12, True)
    attend_pairs(0, 4)

    drain()

    @pl.when(jnp.logical_and(mine, ends))
    def _():
        feed(0).wait_send()
        feed(1).wait_send()

    for copy in halo_copies(0, 1):
        copy.wait_send()

    @pl.when(inner)
    def _():
        for copy in pole_copies(0, 1, 2)(theirs):
            copy.wait_send()

    mate_copy(core).wait_send()
    mask_copy(core).wait_send()
    for j in range(4):
        cols = pl.ds(pl.multiple_of(128 * (4 * (1 - core) + j), 128), 128)
        out_copy(j, block(j)).wait_send()
        out_copy(j, cols).wait_recv()


def per_device(tokens, w_qkv, rel_bias, tile_valid):
    rows, cols, width = tokens.shape
    vmem = pl.BlockSpec(memory_space=pltpu.VMEM)
    hbm = pl.BlockSpec(memory_space=pl.ANY)
    dma = pltpu.SemaphoreType.DMA
    out = pl.pallas_call(
        kernel,
        out_shape=jax.ShapeDtypeStruct((rows * cols, width), jnp.bfloat16),
        in_specs=[hbm, hbm, vmem, pl.BlockSpec(memory_space=pltpu.SMEM)],
        out_specs=vmem,
        scratch_shapes=[
            pltpu.VMEM((Z, D, 128), jnp.bfloat16),
            pltpu.VMEM((SIDE, WIDE, D), jnp.bfloat16),
            pltpu.VMEM((4, 2, 256, 128), jnp.bfloat16),
            pltpu.VMEM((2, 4, SIDE * WIDE, 128), jnp.bfloat16),
            pltpu.VMEM((HEADS, 512), jnp.float32),
            pltpu.VMEM((4, 128, 512), jnp.float32),
            pltpu.VMEM((2, 2, TILE, 20 * WIDE), jnp.float32),
            pltpu.VMEM((4, 128, 128), jnp.bfloat16),
            dma((2 * STRIDE + 4, Z)),
            dma((6, Z)),
            dma((2,)),
            dma((1,)),
            dma((7,)),
            dma((7,)),
            dma((4,)),
            dma((4,)),
            dma((2,)),
            pltpu.SemaphoreType.REGULAR,
            pltpu.SemaphoreType.REGULAR,
            pltpu.SemaphoreType.REGULAR,
        ],
        compiler_params=pltpu.CompilerParams(
            collective_id=0, has_side_effects=True, vmem_limit_bytes=63 << 20
        ),
    )(tokens, w_qkv, jnp.transpose(rel_bias, (1, 0, 2)), tile_valid)
    return out.reshape(rows, cols, width)


def solution(mesh):
    placed = (P("lat", "lon", None), P(None, "lon"), P(), P("lat", "lon", None))
    return jax.shard_map(
        per_device, mesh=mesh, in_specs=placed, out_specs=P("lat", "lon", None), check_vma=False
    )
```

```python
import functools

import jax
import jax.numpy as jnp
from jax import lax
from jax.experimental import pallas as pl
from jax.experimental.pallas import tpu as pltpu
from jax.sharding import PartitionSpec as P

HEADS = 16
HD = 64
D = 1024
TILE = 8
RADIUS = 6
REACH = 2 * RADIUS + 1
ROWS = 256
SIDE = 28
WIDE = 32
NEG = -1e30

X = 4
Y = 8
Z = 12
STRIDE = 2
PART = D // 4
HALF = PART // 2


def remote(src, dst, send_sem, recv_sem, device):
    return pltpu.make_async_remote_copy(
        src_ref=src,
        dst_ref=dst,
        send_sem=send_sem,
        recv_sem=recv_sem,
        device_id=device,
        device_id_type=pl.DeviceIdType.MESH,
    )


def kernel(
    tok_ref,
    w_ref,
    bias_ref,
    flag_ref,
    out_ref,
    wbuf,
    xall,
    qbuf,
    kvbuf,
    lines,
    table,
    masks,
    obuf,
    sends,
    recvs,
    xsends,
    xrecvs,
    hsends,
    hrecvs,
    osends,
    orecvs,
    local,
    token,
    opened,
    reached,
):
    lat = lax.axis_index("lat")
    lon = lax.axis_index("lon")
    core = lat % 2
    x = (lat // 2) % X
    ylo = lat // 8
    yhi = lon // Z
    z = lon % Z
    y = yhi * 4 + ylo
    colour = (x + 2 * y) % 4

    def place(xx, yy, zz):
        return ((yy % 4) * 8 + xx * 2 + core, (yy // 4) * Z + zz)

    ups = [place(x, y, (z + i) % Z) for i in range(1, STRIDE + 1)]
    downs = [place(x, y, (z + Z - i) % Z) for i in range(1, STRIDE + 1)]
    x_up, x_down = place((x + 1) % X, y, z), place((x + X - 1) % X, y, z)
    y_up, y_down = place(x, (y + 1) % Y, z), place(x, (y + Y - 1) % Y, z)
    mate = (lat + 1 - 2 * core, lon)
    east, west = (lon + 1) % (2 * Z), (lon + 2 * Z - 1) % (2 * Z)
    vert = lat + 2 * core - 1
    inner = jnp.logical_and(vert >= 0, vert < ROWS // TILE)
    ends = jnp.logical_or(ylo == 0, ylo == 3)
    far_lo = jnp.where(ylo == 3, 0, 2)
    over = 4 * (1 - yhi)
    feeder = place(x, over + jnp.where(ylo < 2, 3, 0), z)

    def fed(i):
        return place(x, over + far_lo + i, z)

    middle = jnp.where(z // 4 == 1, 1, 0)
    mine = yhi == (core + middle) % 2

    def part(c):
        return pl.ds(pl.multiple_of((c % 4) * PART, PART), PART)

    def first(c):
        return pl.ds(pl.multiple_of((c % 4) * PART, PART), HALF)

    def second(c):
        return pl.ds(pl.multiple_of((c % 4) * PART + HALF, HALF), HALF)

    barrier = pltpu.get_barrier_semaphore()

    def hello(device):
        pl.semaphore_signal(
            barrier, inc=1, device_id=device, device_id_type=pl.DeviceIdType.MESH
        )

    for device in (x_up, x_down, y_up, y_down, mate, feeder):
        hello(device)
    count = 6
    opposite = (lon + Z) % (2 * Z)
    for some, devices in (
        (ends, (fed(0), fed(1))),
        (inner, ((vert, lon),)),
        (z <= Z - 2, (ups[0],)),
        (z <= Z - 3, (ups[1],)),
        (z >= 1, (downs[0],)),
        (z >= 2, (downs[1],)),
        (jnp.logical_and(inner, z < Z - 1), ((vert, east),)),
        (jnp.logical_and(inner, z > 0), ((vert, west),)),
        (z == 0, ((lat, opposite),)),
        (jnp.logical_and(inner, z == 0), ((vert, opposite),)),
    ):
        count = count + jnp.where(some, len(devices), 0)

        @pl.when(some)
        def _():
            for device in devices:
                hello(device)

    mid = 6 + 8 * core
    own_tokens = pltpu.make_async_copy(tok_ref, xall.at[pl.ds(mid, 8), 8:24], local.at[1])
    own_tokens.start()
    own_weights = pltpu.make_async_copy(
        w_ref.at[part(colour)], wbuf.at[z, part(colour)], local.at[0]
    )

    @pl.when(mine)
    def _():
        own_weights.start()

    @pl.when(jnp.logical_not(inner))
    def _():
        xall[pl.ds(22 * core, RADIUS)] = jnp.zeros((RADIUS, WIDE, D), jnp.bfloat16)

    pl.semaphore_wait(barrier, count)

    def feed(i):
        rows = part(x + 2 * (over + far_lo + i))
        return remote(w_ref.at[rows], wbuf.at[z, rows], xsends.at[i], xrecvs.at[0], fed(i))

    @pl.when(jnp.logical_and(mine, ends))
    def _():
        feed(0).start()
        feed(1).start()

    def tell(semaphore, device):
        pl.semaphore_signal(
            semaphore, inc=1, device_id=device, device_id_type=pl.DeviceIdType.MESH
        )

    @pl.when(jnp.logical_and(z > 0, jnp.logical_or(z % 2 == 0, z == Z - 1)))
    def _():
        pl.semaphore_wait(token, 1)

    @pl.when(jnp.logical_and(z % 2 == 0, z < Z - 2))
    def _():
        tell(token, ups[1])

    @pl.when(z == Z - 2)
    def _():
        tell(token, ups[0])
        tell(opened, ups[1])


    @pl.when(z == Z - 1)
    def _():
        tell(opened, ups[0])
        tell(opened, ups[1])
        tell(reached, (lat, east))

        @pl.when(inner)
        def _():
            tell(reached, (vert, east))

    def along(p, rows, kind, landing, device):
        ref = wbuf.at[p, rows]
        return remote(ref, ref, sends.at[kind], recvs.at[landing, p], device)

    def behind(d):
        return (z + Z - d) % Z

    def ahead(d):
        return (z + d) % Z

    def relay_up(d, act):
        p = behind(d)

        @pl.when(jnp.logical_and(d % STRIDE == 0, d < 6))
        def _():
            act(along(p, part(colour), 0, 0, ups[0]))

            @pl.when(d < 4)
            def _():
                act(along(p, part(colour), 1, 0, ups[1]))

            @pl.when(jnp.logical_and(d == 4, p < 6))
            def _():
                act(along(p, part(colour), 1, 0, ups[1]))

    def relay_down(d, act, crossing):
        p = ahead(d)
        for i in range(STRIDE):
            here = (z < i + 1) if crossing else (z >= i + 1)

            @pl.when(jnp.logical_and(here, jnp.logical_and(d % STRIDE == 0, d < 6)))
            def _():
                if i == 0:
                    act(along(p, part(colour), 2, 0, downs[0]))
                else:

                    @pl.when(d < 4)
                    def _():
                        act(along(p, part(colour), 3, 0, downs[1]))

                    @pl.when(jnp.logical_and(d == 4, p >= 6))
                    def _():
                        act(along(p, part(colour), 3, 0, downs[1]))

    def pushes(p):
        kind = 2 * STRIDE
        return [
            along(p, part(colour), kind, 1, x_up),
            along(p, part(colour), kind + 1, 1, x_down),
            along(p, first(colour), kind + 2, 1, y_up),
            along(p, second(colour), kind + 3, 1, y_down),
        ]

    def start(copy):
        copy.start()

    def own_out():
        relay_up(0, start)
        relay_down(0, start, False)
        for copy in pushes(z):
            copy.start()

    def whole_in(p):
        along(p, part(colour), 0, 0, ups[0]).wait_recv()

    def pass_on(i, late):
        d = jnp.where(i < 4, i + 2 - 2 * (i % 2), i + 1)

        @pl.when(jnp.logical_and(d < 6, (d > z) == late))
        def _():
            whole_in(behind(d))
            relay_up(d, start)
            for copy in pushes(behind(d)):
                copy.start()

        @pl.when(jnp.logical_and(d < 6, (z + d >= Z) == late))
        def _():
            whole_in(ahead(d))
            relay_down(d, start, False)
            for copy in pushes(ahead(d)):
                copy.start()

        if late:

            @pl.when(d == 6)
            def _():
                whole_in(behind(d))
                for copy in pushes(behind(d)):
                    copy.start()

    def early_shards():
        def body(i, carry):
            pass_on(i, False)
            return carry

        lax.fori_loop(0, 5, body, 0)

    def late_shards(low, high):
        def body(i, carry):
            pass_on(i, True)
            return carry

        lax.fori_loop(low, high, body, 0)

    def cross_down():
        def body(i, carry):
            relay_down(2 * i, start, True)
            return carry

        lax.fori_loop(0, 3, body, 0)

    def drain():
        def sent(kind, shards, rows):
            ref = wbuf.at[pl.ds(0, shards), pl.ds(0, rows)]
            remote(ref, ref, sends.at[kind], recvs.at[0, 0], x_up).wait_send()

        sent(0, 3, PART)
        sent(2, 3, PART)
        for kind, third in (
            (1, jnp.logical_and(z >= 4, z <= 9)),
            (3, jnp.logical_and(z >= 2, z <= 7)),
        ):

            @pl.when(third)
            def _():
                sent(kind, 3, PART)

            @pl.when(jnp.logical_not(third))
            def _():
                sent(kind, 2, PART)

        sent(4, Z, PART)
        sent(5, Z, PART)
        sent(6, Z, HALF)
        sent(7, Z, HALF)

    def filled(p):
        ref = wbuf.at[p, pl.ds(0, 3 * PART)]
        remote(ref, ref, sends.at[0], recvs.at[1, p], x_up).wait_recv()

    @pl.when(mine)
    def _():
        own_weights.wait()
        own_out()

    edge = 22 * core
    theirs = 22 - 22 * core
    give = 2 * core

    def halo_copies(*which):
        pairs = ((tok_ref.at[:, 8:16], 0, east), (tok_ref.at[:, 0:8], 24, west))
        copies = []
        for k in which:
            src, col, to = pairs[k]
            dst = xall.at[pl.ds(mid, 8), col : col + 8]
            copies.append(remote(src, dst, hsends.at[k], hrecvs.at[k], (lat, to)))
        return copies

    def pole_copies(*which):
        give_rows = pl.ds(give, RADIUS)

        def one(dst_row):
            land = pl.ds(dst_row, RADIUS)
            cuts = ((0, 16, 8, lon), (8, 16, 0, east), (0, 8, 24, west))
            copies = []
            for k in which:
                a, b, col, to = cuts[k]
                src = tok_ref.at[give_rows, a:b]
                dst = xall.at[land, col : col + b - a]
                copies.append(remote(src, dst, hsends.at[2 + k], hrecvs.at[2 + k], (vert, to)))
            return copies

        return one

    def mate_copy(half):
        rows = pl.ds(14 * half, 14)
        return remote(xall.at[rows], xall.at[rows], hsends.at[5], hrecvs.at[5], mate)

    def mask_copy(half):
        return remote(masks.at[half], masks.at[half], hsends.at[6], hrecvs.at[6], mate)

    def halo_west():
        halo_copies(1)[0].start()

        @pl.when(inner)
        def _():
            pole_copies(2)(theirs)[0].start()

    halo_copies(0)[0].start()

    @pl.when(inner)
    def _():
        for copy in pole_copies(0, 1)(theirs):
            copy.start()

    @pl.when(z > 0)
    def _():
        halo_west()

    @pl.when(jnp.logical_not(mine))
    def _():
        rows = part(colour)
        remote(w_ref.at[rows], wbuf.at[z, rows], xsends.at[0], xrecvs.at[0], feeder).wait_recv()
        own_out()

    lane = lax.broadcasted_iota(jnp.int32, (TILE, 20 * WIDE), 1)
    krow = lane // WIDE
    kcol = lane % WIDE
    up = (krow + 2) // TILE
    grow = lat * TILE + krow - RADIUS
    exists = jnp.logical_and(grow >= 0, grow < ROWS)
    for tc in range(2):
        side = kcol // TILE - tc
        level = jnp.full(lane.shape, NEG, jnp.float32)
        for du in range(3):
            for dv in range(3):
                slot = 3 * du + dv
                value = 0.0
                if slot != 4:
                    value = jnp.where(flag_ref[0, tc, slot] > 0, 0.0, NEG)
                level = jnp.where(jnp.logical_and(up == du, side == dv), value, level)
        masks[core, tc] = jnp.where(exists, level, NEG)
    mask_copy(core).start()

    lines[...] = jnp.full(lines.shape, NEG, jnp.float32)
    for a in range(REACH):
        lines[:, WIDE * a : WIDE * a + REACH] = bias_ref[a]
    for h in range(HEADS // 2):
        line = lines[pl.ds(8 * core + h, 1), :]
        spread = jnp.broadcast_to(line, (16, 512))
        for qr in range(4):
            start_row = 64 * (h % 2) + 16 * qr
            table[h // 2, start_row : start_row + 16, :] = pltpu.roll(
                spread, WIDE * qr + 2, 1, stride=1, stride_axis=0
            )

    lane = lax.broadcasted_iota(jnp.int32, (256, 128), 1)

    def project(p):
        j = p % 4
        role = (3 + core - p // 4) % 3

        @pl.when(role == 0)
        def _():
            q = jnp.dot(
                xall[6:22, 8:24, :].reshape(256, D), wbuf[p], preferred_element_type=jnp.float32
            )
            q = q * (1.0 / HD**0.5)
            qbuf[j, 0] = jnp.where(lane < HD, q, 0.0).astype(jnp.bfloat16)
            qbuf[j, 1] = jnp.where(lane < HD, 0.0, q).astype(jnp.bfloat16)

        @pl.when(role > 0)
        def _():
            kvbuf[role - 1, j] = jnp.dot(
                xall[...].reshape(SIDE * WIDE, D), wbuf[p], preferred_element_type=jnp.float32
            ).astype(jnp.bfloat16)

    def consume(i, late):
        d = (i + 1) // 2
        p = jnp.where(i % 2 == 1, behind(d), ahead(d))
        far = jnp.where(i % 2 == 1, d > z, z + d >= Z)

        @pl.when(jnp.logical_or(far, d == 6) == late)
        def _():
            filled(p)
            project(p)

    small = lax.broadcasted_iota(jnp.int32, (64, 128), 1)

    def attend(j, band):
        q = qbuf[j, :, pl.ds(pl.multiple_of(64 * band, 64), 64), :].reshape(128, 128)
        keys = pl.ds(pl.multiple_of(128 * band, 128), 512)
        k = kvbuf[0, j, keys, :]
        v = kvbuf[1, j, keys, :]
        score = lax.dot_general(
            q, k, (((1,), (1,)), ((), ())), preferred_element_type=jnp.float32
        )
        shift = pl.multiple_of(128 * (band % 2), 128)
        mask = masks[band // 2, :, :, pl.ds(shift, 512)]
        score = (score + table[j]).reshape(8, 2, TILE, 512) + mask[None]
        score = score.reshape(128, 512)
        top = jnp.max(score, axis=1, keepdims=True)
        expo = jnp.exp(score - top)
        total = jnp.sum(expo, axis=1, keepdims=True)
        both = jnp.dot(expo.astype(jnp.bfloat16), v, preferred_element_type=jnp.float32)
        both = both * (1.0 / total)
        return jnp.where(small < HD, both[:64], both[64:]).astype(jnp.bfloat16)

    def block(j):
        return pl.ds(pl.multiple_of(128 * (4 * core + j), 128), 128)

    def out_copy(j, cols):
        return remote(obuf.at[j], out_ref.at[:, cols], osends.at[j], orecvs.at[j], mate)

    def heads(i):
        j = (z + jnp.where(i == 0, 0, jnp.where(i == 1, 3, i - 1))) % 4
        for b in range(2):
            obuf[j, 64 * b : 64 * b + 64, :] = attend(j, 2 * (1 - core) + b)
        out_copy(j, block(j)).start()
        for b in range(2):
            out_ref[64 * b : 64 * b + 64, block(j)] = attend(j, 2 * core + b)

    def tokens_in():
        for copy in halo_copies(0, 1):
            copy.wait_recv()

        @pl.when(inner)
        def _():
            for copy in pole_copies(0, 1, 2)(edge):
                copy.wait_recv()

        own_tokens.wait()
        mate_copy(core).start()

    def region_in():
        mate_copy(1 - core).wait_recv()
        mask_copy(1 - core).wait_recv()

    def open_wrap():
        @pl.when(z < STRIDE)
        def _():
            pl.semaphore_wait(opened, STRIDE - z)

            @pl.when(z == 0)
            def _():
                pl.semaphore_wait(reached, 1 + jnp.where(inner, 1, 0))
                halo_west()

            cross_down()

    def project_shards(low, high, late):
        def body(i, carry):
            consume(i, late)
            return carry

        lax.fori_loop(low, high, body, 0)

    def finish_pairs():
        def shard(i, carry):
            consume(i, True)
            return carry

        def body(k, carry):
            lax.fori_loop(jnp.where(k == 0, 1, 8 + k), 9 + k, shard, 0)
            heads(k)
            return carry

        lax.fori_loop(0, 4, body, 0)

    early_shards()
    open_wrap()
    late_shards(0, 2)
    tokens_in()
    late_shards(2, 4)
    region_in()
    project_shards(0, 5, False)
    late_shards(4, 6)
    project_shards(5, 11, False)
    finish_pairs()

    drain()

    @pl.when(jnp.logical_and(mine, ends))
    def _():
        feed(0).wait_send()
        feed(1).wait_send()

    for copy in halo_copies(0, 1):
        copy.wait_send()

    @pl.when(inner)
    def _():
        for copy in pole_copies(0, 1, 2)(theirs):
            copy.wait_send()

    mate_copy(core).wait_send()
    mask_copy(core).wait_send()
    for j in range(4):
        cols = pl.ds(pl.multiple_of(128 * (4 * (1 - core) + j), 128), 128)
        out_copy(j, block(j)).wait_send()
        out_copy(j, cols).wait_recv()


def per_device(tokens, w_qkv, rel_bias, tile_valid):
    rows, cols, width = tokens.shape
    vmem = pl.BlockSpec(memory_space=pltpu.VMEM)
    hbm = pl.BlockSpec(memory_space=pl.ANY)
    dma = pltpu.SemaphoreType.DMA
    out = pl.pallas_call(
        kernel,
        out_shape=jax.ShapeDtypeStruct((rows * cols, width), jnp.bfloat16),
        in_specs=[hbm, hbm, vmem, pl.BlockSpec(memory_space=pltpu.SMEM)],
        out_specs=vmem,
        scratch_shapes=[
            pltpu.VMEM((Z, D, 128), jnp.bfloat16),
            pltpu.VMEM((SIDE, WIDE, D), jnp.bfloat16),
            pltpu.VMEM((4, 2, 256, 128), jnp.bfloat16),
            pltpu.VMEM((2, 4, SIDE * WIDE, 128), jnp.bfloat16),
            pltpu.VMEM((HEADS, 512), jnp.float32),
            pltpu.VMEM((4, 128, 512), jnp.float32),
            pltpu.VMEM((2, 2, TILE, 20 * WIDE), jnp.float32),
            pltpu.VMEM((4, 128, 128), jnp.bfloat16),
            dma((2 * STRIDE + 4,)),
            dma((2, Z)),
            dma((2,)),
            dma((1,)),
            dma((7,)),
            dma((7,)),
            dma((4,)),
            dma((4,)),
            dma((2,)),
            pltpu.SemaphoreType.REGULAR,
            pltpu.SemaphoreType.REGULAR,
            pltpu.SemaphoreType.REGULAR,
        ],
        compiler_params=pltpu.CompilerParams(
            collective_id=0, has_side_effects=True, vmem_limit_bytes=63 << 20
        ),
    )(tokens, w_qkv, jnp.transpose(rel_bias, (1, 0, 2)), tile_valid)
    return out.reshape(rows, cols, width)


def solution(mesh):
    placed = (P("lat", "lon", None), P(None, "lon"), P(), P("lat", "lon", None))
    return jax.shard_map(
        per_device, mesh=mesh, in_specs=placed, out_specs=P("lat", "lon", None), check_vma=False
    )
```

```python
import functools

import jax
import jax.numpy as jnp
from jax import lax
from jax.experimental import pallas as pl
from jax.experimental.pallas import tpu as pltpu
from jax.sharding import PartitionSpec as P

HEADS = 16
HD = 64
D = 1024
TILE = 8
RADIUS = 6
REACH = 2 * RADIUS + 1
ROWS = 256
SIDE = 28
WIDE = 32
NEG = -1e30

X = 4
Y = 8
Z = 12
STRIDE = 2
FAR = 7
PART = D // 4
HALF = PART // 2


def remote(src, dst, send_sem, recv_sem, device):
    return pltpu.make_async_remote_copy(
        src_ref=src,
        dst_ref=dst,
        send_sem=send_sem,
        recv_sem=recv_sem,
        device_id=device,
        device_id_type=pl.DeviceIdType.MESH,
    )


def kernel(
    tok_ref,
    w_ref,
    bias_ref,
    flag_ref,
    out_ref,
    wbuf,
    xall,
    qbuf,
    kvbuf,
    lines,
    table,
    masks,
    obuf,
    sends,
    recvs,
    xsends,
    xrecvs,
    hsends,
    hrecvs,
    osends,
    orecvs,
    local,
    token,
    opened,
    reached,
):
    lat = lax.axis_index("lat")
    lon = lax.axis_index("lon")
    core = lat % 2
    x = (lat // 2) % X
    ylo = lat // 8
    yhi = lon // Z
    z = lon % Z
    y = yhi * 4 + ylo
    colour = (x + 2 * y) % 4

    def place(xx, yy, zz):
        return ((yy % 4) * 8 + xx * 2 + core, (yy // 4) * Z + zz)

    ups = [place(x, y, (z + i) % Z) for i in range(1, STRIDE + 1)]
    downs = [place(x, y, (z + Z - i) % Z) for i in range(1, STRIDE + 1)]
    x_up, x_down = place((x + 1) % X, y, z), place((x + X - 1) % X, y, z)
    y_up, y_down = place(x, (y + 1) % Y, z), place(x, (y + Y - 1) % Y, z)
    mate = (lat + 1 - 2 * core, lon)
    east, west = (lon + 1) % (2 * Z), (lon + 2 * Z - 1) % (2 * Z)
    vert = lat + 2 * core - 1
    inner = jnp.logical_and(vert >= 0, vert < ROWS // TILE)
    ends = jnp.logical_or(ylo == 0, ylo == 3)
    far_lo = jnp.where(ylo == 3, 0, 2)
    over = 4 * (1 - yhi)
    feeder = place(x, over + jnp.where(ylo < 2, 3, 0), z)

    def fed(i):
        return place(x, over + far_lo + i, z)

    middle = jnp.where(z // 4 == 1, 1, 0)
    owner = (core + middle) % 2
    mine = yhi == owner
    up_lacks = ((y + 1) % Y) // 4 != owner
    down_lacks = ((y + Y - 1) % Y) // 4 != owner

    def part(c):
        return pl.ds(pl.multiple_of((c % 4) * PART, PART), PART)

    def first(c):
        return pl.ds(pl.multiple_of((c % 4) * PART, PART), HALF)

    def second(c):
        return pl.ds(pl.multiple_of((c % 4) * PART + HALF, HALF), HALF)

    barrier = pltpu.get_barrier_semaphore()

    def hello(device):
        pl.semaphore_signal(
            barrier, inc=1, device_id=device, device_id_type=pl.DeviceIdType.MESH
        )

    for device in (x_up, x_down, y_up, y_down, mate, feeder):
        hello(device)
    count = 6
    opposite = (lon + Z) % (2 * Z)
    for some, devices in (
        (ends, (fed(0), fed(1))),
        (inner, ((vert, lon),)),
        (z <= Z - 2, (ups[0],)),
        (z <= Z - 3, (ups[1],)),
        (z >= 1, (downs[0],)),
        (z >= 2, (downs[1],)),
        (jnp.logical_and(inner, z < Z - 1), ((vert, east),)),
        (jnp.logical_and(inner, z > 0), ((vert, west),)),
        (z == 0, ((lat, opposite),)),
        (jnp.logical_and(inner, z == 0), ((vert, opposite),)),
    ):
        count = count + jnp.where(some, len(devices), 0)

        @pl.when(some)
        def _():
            for device in devices:
                hello(device)

    mid = 6 + 8 * core
    own_tokens = pltpu.make_async_copy(tok_ref, xall.at[pl.ds(mid, 8), 8:24], local.at[1])
    own_tokens.start()
    own_weights = pltpu.make_async_copy(
        w_ref, wbuf.at[z], local.at[0]
    )

    @pl.when(mine)
    def _():
        own_weights.start()

    @pl.when(jnp.logical_not(inner))
    def _():
        xall[pl.ds(22 * core, RADIUS)] = jnp.zeros((RADIUS, WIDE, D), jnp.bfloat16)

    pl.semaphore_wait(barrier, count)

    def feed(i):
        rows = part(x + 2 * (over + far_lo + i))
        return remote(w_ref.at[rows], wbuf.at[z, rows], xsends.at[i], xrecvs.at[0], fed(i))

    @pl.when(jnp.logical_and(mine, ends))
    def _():
        feed(0).start()
        feed(1).start()

    def tell(semaphore, device):
        pl.semaphore_signal(
            semaphore, inc=1, device_id=device, device_id_type=pl.DeviceIdType.MESH
        )

    @pl.when(jnp.logical_and(z > 0, jnp.logical_or(z % 2 == 0, z == Z - 1)))
    def _():
        pl.semaphore_wait(token, 1)

    @pl.when(jnp.logical_and(z % 2 == 0, z < Z - 2))
    def _():
        tell(token, ups[1])

    @pl.when(z == Z - 2)
    def _():
        tell(token, ups[0])
        tell(opened, ups[1])


    @pl.when(z == Z - 1)
    def _():
        tell(opened, ups[0])
        tell(opened, ups[1])
        tell(reached, (lat, east))

        @pl.when(inner)
        def _():
            tell(reached, (vert, east))

    def along(p, rows, kind, landing, device):
        ref = wbuf.at[p, rows]
        return remote(ref, ref, sends.at[kind], recvs.at[landing, p], device)

    def behind(d):
        return (z + Z - d) % Z

    def ahead(d):
        return (z + d) % Z

    def goes_up(d, i):
        inside = jnp.logical_and(d <= z, z + i < Z)
        return jnp.logical_and(d % STRIDE == 0, d + i <= jnp.where(inside, FAR, 5))

    def goes_down(d, i):
        inside = jnp.logical_and(z + d < Z, z >= i)
        return jnp.logical_and(d % STRIDE == 0, d + i <= jnp.where(inside, 6, 11 - FAR))

    def relay_up(d):
        for i in (1, 2):

            @pl.when(goes_up(d, i))
            def _():
                along(behind(d), part(colour), i - 1, 0, ups[i - 1]).start()

    def relay_down(d, crossing):
        for i in (1, 2):
            here = (z < i) if crossing else (z >= i)

            @pl.when(jnp.logical_and(here, goes_down(d, i)))
            def _():
                along(ahead(d), part(colour), i + 1, 0, downs[i - 1]).start()

    def pushes(p):
        kind = 2 * STRIDE
        return [
            along(p, part(colour), kind, 1, x_up),
            along(p, part(colour), kind + 1, 1, x_down),
            along(p, first(colour), kind + 2, 1, y_up),
            along(p, second(colour), kind + 3, 1, y_down),
        ]

    def own_out():
        relay_up(0)
        relay_down(0, False)
        own = pushes(z)

        @pl.when(jnp.logical_not(mine))
        def _():
            own[0].start()
            own[1].start()

        @pl.when(up_lacks)
        def _():
            own[2].start()

        @pl.when(down_lacks)
        def _():
            own[3].start()

    def whole_in(p):
        along(p, part(colour), 0, 0, ups[0]).wait_recv()

    def from_low(d, late):
        if late:
            return jnp.logical_and(d > z, d < 6)
        return jnp.logical_and(d <= z, d <= FAR)

    def from_high(d, late):
        crossed = jnp.logical_and(z + d >= Z, d <= 11 - FAR)
        if late:
            return jnp.logical_or(crossed, jnp.logical_and(d == 6, z < 6))
        return jnp.logical_and(z + d < Z, d < 6)

    def pass_on(i, late):
        d = jnp.where(i == 4, 5, jnp.where(i == 5, 6, i + 2 - 2 * (i % 2))) if late else (
            i + 2 - 2 * (i % 2)
        )

        @pl.when(from_low(d, late))
        def _():
            whole_in(behind(d))
            relay_up(d)
            for copy in pushes(behind(d)):
                copy.start()

        @pl.when(from_high(d, late))
        def _():
            whole_in(ahead(d))
            relay_down(d, False)
            for copy in pushes(ahead(d)):
                copy.start()

    def early_shards():
        def body(i, carry):
            pass_on(i, False)
            return carry

        lax.fori_loop(0, FAR + FAR % 2, body, 0)

    def late_shards(low, high):
        def body(i, carry):
            pass_on(i, True)
            return carry

        lax.fori_loop(low, high, body, 0)

    def cross_down():
        def body(i, carry):
            relay_down(2 * i, True)
            return carry

        lax.fori_loop(0, 3, body, 0)

    def drain():
        def sent(kind, shards, rows):
            ref = wbuf.at[pl.ds(0, shards), pl.ds(0, rows)]
            remote(ref, ref, sends.at[kind], recvs.at[0, 0], x_up).wait_send()

        for kind, goes, i in ((0, goes_up, 1), (1, goes_up, 2), (2, goes_down, 1), (3, goes_down, 2)):
            number = 0
            for d in (0, 2, 4, 6, 8):
                number = number + jnp.where(goes(d, i), 1, 0)
            for n in range(1, 6):

                @pl.when(number == n)
                def _():
                    sent(kind, n, PART)

        lacks = jnp.logical_not(mine)
        for kind, some, rows in (
            (4, lacks, PART),
            (5, lacks, PART),
            (6, up_lacks, HALF),
            (7, down_lacks, HALF),
        ):

            @pl.when(some)
            def _():
                sent(kind, Z, rows)

            @pl.when(jnp.logical_not(some))
            def _():
                sent(kind, Z - 1, rows)

    def filled(p):
        ref = wbuf.at[p, pl.ds(0, 3 * PART)]
        remote(ref, ref, sends.at[0], recvs.at[1, p], x_up).wait_recv()

    @pl.when(mine)
    def _():
        own_weights.wait()
        own_out()

    edge = 22 * core
    theirs = 22 - 22 * core
    give = 2 * core

    def halo_copies(*which):
        pairs = ((tok_ref.at[:, 8:16], 0, east), (tok_ref.at[:, 0:8], 24, west))
        copies = []
        for k in which:
            src, col, to = pairs[k]
            dst = xall.at[pl.ds(mid, 8), col : col + 8]
            copies.append(remote(src, dst, hsends.at[k], hrecvs.at[k], (lat, to)))
        return copies

    def pole_copies(*which):
        give_rows = pl.ds(give, RADIUS)

        def one(dst_row):
            land = pl.ds(dst_row, RADIUS)
            cuts = ((0, 16, 8, lon), (8, 16, 0, east), (0, 8, 24, west))
            copies = []
            for k in which:
                a, b, col, to = cuts[k]
                src = tok_ref.at[give_rows, a:b]
                dst = xall.at[land, col : col + b - a]
                copies.append(remote(src, dst, hsends.at[2 + k], hrecvs.at[2 + k], (vert, to)))
            return copies

        return one

    def mate_copy(half):
        rows = pl.ds(14 * half, 14)
        return remote(xall.at[rows], xall.at[rows], hsends.at[5], hrecvs.at[5], mate)

    def mask_copy(half):
        return remote(masks.at[half], masks.at[half], hsends.at[6], hrecvs.at[6], mate)

    def halo_west():
        halo_copies(1)[0].start()

        @pl.when(inner)
        def _():
            pole_copies(2)(theirs)[0].start()

    halo_copies(0)[0].start()

    @pl.when(inner)
    def _():
        for copy in pole_copies(0, 1)(theirs):
            copy.start()

    @pl.when(z > 0)
    def _():
        halo_west()

    @pl.when(jnp.logical_not(mine))
    def _():
        rows = part(colour)
        remote(w_ref.at[rows], wbuf.at[z, rows], xsends.at[0], xrecvs.at[0], feeder).wait_recv()
        own_out()

    lane = lax.broadcasted_iota(jnp.int32, (TILE, 20 * WIDE), 1)
    krow = lane // WIDE
    kcol = lane % WIDE
    up = (krow + 2) // TILE
    grow = lat * TILE + krow - RADIUS
    exists = jnp.logical_and(grow >= 0, grow < ROWS)
    for tc in range(2):
        side = kcol // TILE - tc
        level = jnp.full(lane.shape, NEG, jnp.float32)
        for du in range(3):
            for dv in range(3):
                slot = 3 * du + dv
                value = 0.0
                if slot != 4:
                    value = jnp.where(flag_ref[0, tc, slot] > 0, 0.0, NEG)
                level = jnp.where(jnp.logical_and(up == du, side == dv), value, level)
        masks[core, tc] = jnp.where(exists, level, NEG)
    mask_copy(core).start()

    lines[...] = jnp.full(lines.shape, NEG, jnp.float32)
    for a in range(REACH):
        lines[:, WIDE * a : WIDE * a + REACH] = bias_ref[a]
    for h in range(HEADS // 2):
        line = lines[pl.ds(8 * core + h, 1), :]
        spread = jnp.broadcast_to(line, (16, 512))
        for qr in range(4):
            start_row = 64 * (h % 2) + 16 * qr
            table[h // 2, start_row : start_row + 16, :] = pltpu.roll(
                spread, WIDE * qr + 2, 1, stride=1, stride_axis=0
            )

    lane = lax.broadcasted_iota(jnp.int32, (256, 128), 1)

    def project(p):
        j = p % 4
        role = (3 + core - p // 4) % 3

        @pl.when(role == 0)
        def _():
            q = jnp.dot(
                xall[6:22, 8:24, :].reshape(256, D), wbuf[p], preferred_element_type=jnp.float32
            )
            q = q * (1.0 / HD**0.5)
            qbuf[j, 0] = jnp.where(lane < HD, q, 0.0).astype(jnp.bfloat16)
            qbuf[j, 1] = jnp.where(lane < HD, 0.0, q).astype(jnp.bfloat16)

        @pl.when(role > 0)
        def _():
            kvbuf[role - 1, j] = jnp.dot(
                xall[...].reshape(SIDE * WIDE, D), wbuf[p], preferred_element_type=jnp.float32
            ).astype(jnp.bfloat16)

    def consume(i, late):
        d = (i + 1) // 2
        p = jnp.where(i % 2 == 1, behind(d), ahead(d))

        @pl.when(jnp.where(i % 2 == 1, from_low(d, late), from_high(d, late)))
        def _():
            @pl.when(jnp.logical_not(jnp.logical_and(mine, p == z)))
            def _():
                filled(p)

            project(p)

    small = lax.broadcasted_iota(jnp.int32, (64, 128), 1)

    def attend(j, band):
        q = qbuf[j, :, pl.ds(pl.multiple_of(64 * band, 64), 64), :].reshape(128, 128)
        keys = pl.ds(pl.multiple_of(128 * band, 128), 512)
        k = kvbuf[0, j, keys, :]
        v = kvbuf[1, j, keys, :]
        score = lax.dot_general(
            q, k, (((1,), (1,)), ((), ())), preferred_element_type=jnp.float32
        )
        shift = pl.multiple_of(128 * (band % 2), 128)
        mask = masks[band // 2, :, :, pl.ds(shift, 512)]
        score = (score + table[j]).reshape(8, 2, TILE, 512) + mask[None]
        score = score.reshape(128, 512)
        top = jnp.max(score, axis=1, keepdims=True)
        expo = jnp.exp(score - top)
        total = jnp.sum(expo, axis=1, keepdims=True)
        both = jnp.dot(expo.astype(jnp.bfloat16), v, preferred_element_type=jnp.float32)
        both = both * (1.0 / total)
        return jnp.where(small < HD, both[:64], both[64:]).astype(jnp.bfloat16)

    def block(j):
        return pl.ds(pl.multiple_of(128 * (4 * core + j), 128), 128)

    def out_copy(j, cols):
        return remote(obuf.at[j], out_ref.at[:, cols], osends.at[j], orecvs.at[j], mate)

    def heads(i):
        j = (z + jnp.where(i == 0, 0, jnp.where(i == 1, 3, i - 1))) % 4
        for b in range(2):
            obuf[j, 64 * b : 64 * b + 64, :] = attend(j, 2 * (1 - core) + b)
        out_copy(j, block(j)).start()
        for b in range(2):
            out_ref[64 * b : 64 * b + 64, block(j)] = attend(j, 2 * core + b)

    def tokens_in():
        for copy in halo_copies(0, 1):
            copy.wait_recv()

        @pl.when(inner)
        def _():
            for copy in pole_copies(0, 1, 2)(edge):
                copy.wait_recv()

        own_tokens.wait()
        mate_copy(core).start()

    def region_in():
        mate_copy(1 - core).wait_recv()
        mask_copy(1 - core).wait_recv()

    def open_wrap():
        @pl.when(z < STRIDE)
        def _():
            pl.semaphore_wait(opened, STRIDE - z)

            @pl.when(z == 0)
            def _():
                pl.semaphore_wait(reached, 1 + jnp.where(inner, 1, 0))
                halo_west()

            cross_down()

    def project_shards(low, high, late):
        def body(i, carry):
            consume(i, late)
            return carry

        lax.fori_loop(low, high, body, 0)

    def finish_pairs():
        def shard(i, carry):
            consume(i, True)
            return carry

        def body(k, carry):
            low = jnp.where(k == 0, 1, 8 + k)
            lax.fori_loop(low, 9 + k + k // 3, shard, 0)
            heads(k)
            return carry

        lax.fori_loop(0, 4, body, 0)

    early_shards()
    open_wrap()
    late_shards(0, 2)
    tokens_in()
    late_shards(2, 4)
    region_in()
    project_shards(0, 5, False)
    late_shards(4, 6)
    project_shards(5, 2 * FAR, False)
    finish_pairs()

    drain()

    @pl.when(jnp.logical_and(mine, ends))
    def _():
        feed(0).wait_send()
        feed(1).wait_send()

    for copy in halo_copies(0, 1):
        copy.wait_send()

    @pl.when(inner)
    def _():
        for copy in pole_copies(0, 1, 2)(theirs):
            copy.wait_send()

    mate_copy(core).wait_send()
    mask_copy(core).wait_send()
    for j in range(4):
        cols = pl.ds(pl.multiple_of(128 * (4 * (1 - core) + j), 128), 128)
        out_copy(j, block(j)).wait_send()
        out_copy(j, cols).wait_recv()


def per_device(tokens, w_qkv, rel_bias, tile_valid):
    rows, cols, width = tokens.shape
    vmem = pl.BlockSpec(memory_space=pltpu.VMEM)
    hbm = pl.BlockSpec(memory_space=pl.ANY)
    dma = pltpu.SemaphoreType.DMA
    out = pl.pallas_call(
        kernel,
        out_shape=jax.ShapeDtypeStruct((rows * cols, width), jnp.bfloat16),
        in_specs=[hbm, hbm, vmem, pl.BlockSpec(memory_space=pltpu.SMEM)],
        out_specs=vmem,
        scratch_shapes=[
            pltpu.VMEM((Z, D, 128), jnp.bfloat16),
            pltpu.VMEM((SIDE, WIDE, D), jnp.bfloat16),
            pltpu.VMEM((4, 2, 256, 128), jnp.bfloat16),
            pltpu.VMEM((2, 4, SIDE * WIDE, 128), jnp.bfloat16),
            pltpu.VMEM((HEADS, 512), jnp.float32),
            pltpu.VMEM((4, 128, 512), jnp.float32),
            pltpu.VMEM((2, 2, TILE, 20 * WIDE), jnp.float32),
            pltpu.VMEM((4, 128, 128), jnp.bfloat16),
            dma((2 * STRIDE + 4,)),
            dma((2, Z)),
            dma((2,)),
            dma((1,)),
            dma((7,)),
            dma((7,)),
            dma((4,)),
            dma((4,)),
            dma((2,)),
            pltpu.SemaphoreType.REGULAR,
            pltpu.SemaphoreType.REGULAR,
            pltpu.SemaphoreType.REGULAR,
        ],
        compiler_params=pltpu.CompilerParams(
            collective_id=0, has_side_effects=True, vmem_limit_bytes=63 << 20
        ),
    )(tokens, w_qkv, jnp.transpose(rel_bias, (1, 0, 2)), tile_valid)
    return out.reshape(rows, cols, width)


def solution(mesh):
    placed = (P("lat", "lon", None), P(None, "lon"), P(), P("lat", "lon", None))
    return jax.shard_map(
        per_device, mesh=mesh, in_specs=placed, out_specs=P("lat", "lon", None), check_vma=False
    )
```
